256 devices in a mesh: slab: 8 (over z_lo, core), corpus: 32 (over x, z_hi, y).
Axes of the slice: x: 4, y: 4, z: 8 (z_hi: 2, z_lo: 4; z = z_hi * 4 + z_lo), core: 2. Of those that a mesh axis runs over, the one named last changes fastest.
Arguments:
- vectors: bfloat16 [524288, 128], P(('slab', 'corpus')), parts along dimension 0, may hold values from -1.796875 to 1.796875
- docs: int32 [524288], P(('slab', 'corpus')), parts along dimension 0, may hold values from 0 to 63
- prior: float32 [524288], P(('slab', 'corpus')), parts along dimension 0, may hold values from 0.5 to 3
Outputs:
- best: float32 [524288], P(('slab', 'corpus')), parts along dimension 0
The draws below stay inside these ranges and needn't reach their ends.
There are 8 independent parts, one for each index of `slab`. The reference program is written for one: setup_inputs(seed, part) draws one part's arguments, and reference() takes and returns one part's arrays. A program takes and returns all parts, laid end to end along the dimension named above; each array names one. Nothing has to cross between parts.
All inputs are finite; a program needn't handle non-finite values.
Results may differ from the reference program's by a relative error of at most 0.0003.
Values may be sent and summed in bfloat16 or wider, within the bound.
A program may use at most 128 MiB of HBM per device.

```python
import jax
import jax.numpy as jnp
from jax import lax

DIM = 128
TOK_DEV = 2048
ROUNDS = 4
DOCS = 64
TOKENS = 65536
N_CORPUS = 32


def touch_ends(values, key, least, largest):
    shape = values.shape
    spot = [jax.random.randint(jax.random.fold_in(key, axis), (), 0, shape[axis]) for axis in range(len(shape))]
    values = values.at[tuple(spot)].set(least)
    longest = shape.index(max(shape))
    spot[longest] = (spot[longest] + 1) % shape[longest]
    return values.at[tuple(spot)].set(largest)


def block_levels(own_key, dims, pieces, least, high):
    gain, own = 1.0, jax.random.fold_in(own_key, 6)
    for position, blocks in pieces:
        draws = jnp.exp(jax.random.uniform(jax.random.fold_in(own, position), (blocks,), jnp.float32, least / len(pieces), high / len(pieces)))
        gain = gain * jnp.repeat(draws, dims[position] // blocks).reshape([-1 if axis == position else 1 for axis in range(len(dims))])
    return gain


def scatter_about(own_key, dims, spread, reach, pieces=(), kind=jnp.bfloat16):
    loudness = block_levels(own_key, dims, pieces, -0.22, 0.18) if pieces else 1.0
    values = jax.random.normal(own_key, dims, jnp.float32) * spread * loudness
    return jnp.minimum(jnp.maximum(values, -reach), reach).astype(kind)


def setup_inputs(seed: int = 0, part: int = 0) -> dict:
    key_of = jax.random.split(jax.random.key(seed), 4)
    part_splits = jax.random.split(jax.random.fold_in(key_of[3], part), 4)
    return {
        "vectors": scatter_about(part_splits[0], (TOKENS, DIM), (DIM ** -0.25), 1.796875, ((0, 32),)),
        "docs": touch_ends(jax.random.randint(part_splits[1], (TOKENS,), 0, DOCS), jax.random.fold_in(part_splits[1], 1), 0, DOCS - 1).astype(jnp.int32),
        "prior": jnp.clip(0.5 + 2.5 * jax.random.uniform(part_splits[2], (TOKENS,), jnp.float32) ** block_levels(part_splits[2], (TOKENS,), ((0, 32),), -0.2, 0.2), 0.5, 3.0),
    }


NEG = -1e30


def one_tile(args):
    left, left_tags, right, right_tags = args
    scores = jnp.dot(left, right.T, precision=lax.Precision.HIGHEST)
    scores = jnp.where(left_tags[:, None] == right_tags[None, :], NEG, scores)
    return jnp.max(scores, axis=1), jnp.max(scores, axis=0)


def reference(vectors, docs, prior):
    blocks = vectors.astype(jnp.float32).reshape(N_CORPUS, TOK_DEV, DIM)
    labels = docs.reshape(N_CORPUS, TOK_DEV)
    best = prior.reshape(N_CORPUS, TOK_DEV)
    for dist in range(1, ROUNDS + 1):
        others = jnp.roll(blocks, dist, axis=0)
        other_labels = jnp.roll(labels, dist, axis=0)
        rowmax, colmax = lax.map(one_tile, (blocks, labels, others, other_labels))
        best = jnp.maximum(best, rowmax)
        best = jnp.maximum(best, jnp.roll(colmax, -dist, axis=0))
    return best.reshape(TOKENS)
```

```python
import functools

import jax
import jax.numpy as jnp
from jax import lax
from jax.experimental import pallas as pl
from jax.experimental.pallas import tpu as pltpu
from jax.sharding import PartitionSpec as P

MESH = pl.DeviceIdType.MESH
NEG = -1e30
TOK = 2048
DIM = 128
LANES = 128
TAG_ROWS = TOK // LANES
Z_PIECES = 8
Z_ROWS = TOK // Z_PIECES
Y_PIECES = 4
Y_ROWS = TOK // Y_PIECES
BODY = 512
FIRST, SECOND = 4, 5


def kernel(
    v_ref, d_ref, o_ref,
    blocks, tags, wide, rows, cols, res, ret,
    own_sem, a_send, a_recv, b_send, b_recv, c_send, c_recv, d_send, d_recv,
    ta_send, ta_recv, tb_send, tb_recv, tc_send, tc_recv, td_send, td_recv,
    z_send, z_recv, r_send, r_recv, tz_send, tz_recv, tr_send, tr_recv,
    m_send, m_recv,
):
    slab, corpus = lax.axis_index("slab"), lax.axis_index("corpus")
    x, zh, y = corpus // 8, (corpus // 4) % 2, corpus % 4
    core = slab % 2
    takes = (zh + core) % 2 == 1
    gives = (zh + core) % 2 == 0

    def place(px, pz, py):
        return (slab, ((px + 4) % 4) * 8 + pz * 4 + (py + 4) % 4)

    other = 1 - zh
    dx = 1 - 2 * zh
    odx = 1 - 2 * other
    mates = [place(x, zh, y + k) for k in (1, 2, 3)]
    recv_greets = mates + [place(x + 1, zh, y), place(x - 1, zh, y), place(x, other, y), place(x - dx, other, y)]
    send_greets = mates + [place(x, other, y), place(x + odx, other, y)]
    barrier = pltpu.get_barrier_semaphore()

    def hello(ids):
        for to in ids:
            pl.semaphore_signal(barrier, inc=1, device_id=to, device_id_type=MESH)
        pl.semaphore_wait(barrier, len(ids))

    up, two, down = (y + 1) % 4, (y + 2) % 4, (y + 3) % 4

    def remote(src, dst, send, recv, to):
        return pltpu.make_async_remote_copy(
            src_ref=src, dst_ref=dst, send_sem=send, recv_sem=recv, device_id=to, device_id_type=MESH
        )

    def span(k, n):
        return pl.ds(k * n, n)

    def a_copy(c):
        return remote(v_ref.at[span(c, Y_ROWS)], blocks.at[y, span(c, Y_ROWS)], a_send.at[c], a_recv.at[c], mates[2])

    def c_copy(c):
        return remote(
            blocks.at[up, span(c, Y_ROWS)], blocks.at[up, span(c, Y_ROWS)], c_send.at[c], c_recv.at[c], mates[2]
        )

    def z_copy(j):
        return remote(
            v_ref.at[span(j, Z_ROWS)], blocks.at[FIRST, span(j, Z_ROWS)], z_send.at[j], z_recv.at[j], place(x, other, y)
        )

    def r_copy(j):
        return remote(
            blocks.at[FIRST, span(j, Z_ROWS)], blocks.at[SECOND, span(j, Z_ROWS)], r_send.at[j], r_recv.at[j],
            place(x + dx, zh, y),
        )

    b_copy = remote(v_ref, blocks.at[y], b_send, b_recv, mates[0])
    d_copy = remote(v_ref, blocks.at[y], d_send, d_recv, mates[1])
    ta_copy = remote(d_ref, tags.at[y], ta_send, ta_recv, mates[2])
    tb_copy = remote(d_ref, tags.at[y], tb_send, tb_recv, mates[0])
    tc_copy = remote(tags.at[up], tags.at[up], tc_send, tc_recv, mates[2])
    td_copy = remote(d_ref, tags.at[y], td_send, td_recv, mates[1])
    tz_copy = remote(d_ref, tags.at[FIRST], tz_send, tz_recv, place(x, other, y))
    tr_copy = remote(tags.at[FIRST], tags.at[SECOND], tr_send, tr_recv, place(x + dx, zh, y))
    own_v = pltpu.make_async_copy(v_ref, blocks.at[y], own_sem.at[0])
    own_d = pltpu.make_async_copy(d_ref, tags.at[y], own_sem.at[1])

    def widen(b):
        eye = lax.broadcasted_iota(jnp.int32, (LANES, LANES), 0) == lax.broadcasted_iota(jnp.int32, (LANES, LANES), 1)
        ones = jnp.ones((LANES, LANES), jnp.bfloat16)
        labels = tags[b].astype(jnp.float32)
        for q in range(TAG_ROWS):
            line = jnp.broadcast_to(labels[q : q + 1, :], (LANES, LANES))
            spread = jnp.where(eye, line, 0.0).astype(jnp.bfloat16)
            wide[b, q * LANES : (q + 1) * LANES, :] = jnp.dot(spread, ones, preferred_element_type=jnp.float32)

    def tile(left, start, right):
        spot = pl.ds(pl.multiple_of(start, BODY), BODY)
        scores = lax.dot_general(
            blocks[left, spot, :], blocks[right], (((1,), (1,)), ((), ())), preferred_element_type=jnp.float32
        )
        marks = wide[left, spot, :]
        labels = tags[right].astype(jnp.float32)
        best = rows[left, spot, :]
        for q in range(TAG_ROWS):
            part = scores[:, q * LANES : (q + 1) * LANES]
            part = jnp.where(marks == labels[q : q + 1, :], NEG, part)
            best = jnp.maximum(best, part)
            peak = jnp.max(part.reshape(BODY // 8, 8, LANES), axis=0)
            cols[right, :, q * LANES : (q + 1) * LANES] = jnp.maximum(
                cols[right, :, q * LANES : (q + 1) * LANES], peak
            )
        rows[left, spot, :] = best

    def tiles(left, start, count, right):
        @pl.loop(0, count)
        def _(k):
            tile(left, start + k * BODY, right)

    def settle(b, from_rows, from_cols):
        for q in range(TAG_ROWS):
            part = slice(q * LANES, (q + 1) * LANES)
            best = jnp.full((1, LANES), NEG, jnp.float32)
            if from_rows:
                best = jnp.max(rows[b, part, :].T, axis=0, keepdims=True)
            if from_cols:
                best = jnp.maximum(best, jnp.max(cols[b, :, part], axis=0, keepdims=True))
            res[b, q : q + 1, :] = best

    def clear():
        @pl.loop(0, 6)
        def _(b):
            rows[b] = jnp.full((TOK, LANES), NEG, jnp.float32)

        @pl.loop(0, 4)
        def _(b):
            cols[b] = jnp.full((8, TOK), NEG, jnp.float32)

    late = jnp.where(y < 2, two, y)
    early = jnp.where(y < 2, y, two)
    late_start = jnp.where(y < 2, 0, TOK // 2)

    def message(b, slot, sem, to):
        return remote(res.at[b], ret.at[slot], m_send.at[sem], m_recv.at[slot], to)

    @pl.when(takes)
    def _():
        own_v.start()
        own_d.start()
        hello(recv_greets)
        ta_copy.start()
        for c in range(Y_PIECES):
            a_copy(c).start()
        tb_copy.start()
        b_copy.start()
        clear()
        own_v.wait()
        own_d.wait()
        widen(y)

        def on_a(c):
            if c == 0:
                ta_copy.wait_recv()
                tc_copy.start()
                widen(up)
            a_copy(c).wait_recv()
            c_copy(c).start()
            tile(up, c * Y_ROWS, y)

        def on_z(j):
            if j == 0:
                tz_copy.wait_recv()
                tr_copy.start()
                widen(FIRST)
            z_copy(j).wait_recv()
            r_copy(j).start()
            if j % 2 == 1:
                tile(FIRST, (j // 2) * BODY, y)

        on_a(0)
        on_a(1)
        on_z(0)
        on_a(2)
        on_z(1)
        on_a(3)
        for j in range(2, Z_PIECES):
            on_z(j)
        tr_copy.wait_recv()
        widen(SECOND)
        for j in range(Z_PIECES):
            r_copy(j).wait_recv()
        tiles(SECOND, 0, TOK // BODY, y)
        minus = jnp.where(zh == 1, FIRST, SECOND)
        plus = jnp.where(zh == 1, SECOND, FIRST)
        tiles(jnp.where(up > y, plus, minus), 0, TOK // BODY, up)
        tc_copy.wait_recv()
        for c in range(Y_PIECES):
            c_copy(c).wait_recv()
        tiles(jnp.where(two > y, plus, minus), 0, TOK // BODY, two)
        tb_copy.wait_recv()
        b_copy.wait_recv()
        tiles(jnp.where(down > y, plus, minus), 0, TOK // BODY, down)
        settle(FIRST, True, False)
        message(FIRST, 0, 3, place(x, other, y)).start()
        settle(SECOND, True, False)
        message(SECOND, 1, 4, place(x - dx, other, y)).start()
        settle(down, False, True)
        message(down, 0, 0, mates[2]).start()
        settle(up, True, True)
        message(up, 2, 1, mates[0]).start()
        widen(two)
        tiles(late, late_start, TOK // 2 // BODY, early)
        settle(two, True, True)
        message(two, 1, 2, mates[1]).start()
        settle(y, True, True)
        for slot in range(3):
            message(y, slot, slot, mates[slot]).wait_recv()
        best = res[y]
        for slot in range(3):
            best = jnp.maximum(best, ret[slot])
        o_ref[...] = best
        ta_copy.wait_send()
        tb_copy.wait_send()
        tc_copy.wait_send()
        tr_copy.wait_send()
        b_copy.wait_send()
        for c in range(Y_PIECES):
            a_copy(c).wait_send()
            c_copy(c).wait_send()
        for j in range(Z_PIECES):
            r_copy(j).wait_send()
        for sem in range(5):
            message(y, 0, sem, mates[0]).wait_send()

    @pl.when(gives)
    def _():
        own_v.start()
        own_d.start()
        hello(send_greets)
        tz_copy.start()
        for j in range(Z_PIECES):
            z_copy(j).start()
        tb_copy.start()
        b_copy.start()
        td_copy.start()
        d_copy.start()
        clear()
        own_v.wait()
        own_d.wait()
        widen(y)
        tb_copy.wait_recv()
        widen(down)
        b_copy.wait_recv()
        tiles(down, 0, TOK // BODY, y)
        settle(down, True, False)
        message(down, 2, 0, mates[2]).start()
        td_copy.wait_recv()
        widen(two)
        d_copy.wait_recv()
        tiles(late, late_start, TOK // 2 // BODY, early)
        settle(two, True, True)
        message(two, 3, 1, mates[1]).start()
        settle(y, True, True)
        best = res[y]
        for slot in (2, 3, 0, 1):
            message(y, slot, 0, mates[0]).wait_recv()
            best = jnp.maximum(best, ret[slot])
        o_ref[...] = best
        tz_copy.wait_send()
        tb_copy.wait_send()
        td_copy.wait_send()
        b_copy.wait_send()
        d_copy.wait_send()
        for j in range(Z_PIECES):
            z_copy(j).wait_send()
        for sem in range(2):
            message(y, 0, sem, mates[0]).wait_send()


def per_device(vectors, docs, prior):
    dma = pltpu.SemaphoreType.DMA
    pair = [dma, dma]
    found = pl.pallas_call(
        kernel,
        out_shape=jax.ShapeDtypeStruct((TAG_ROWS, LANES), jnp.float32),
        in_specs=[pl.BlockSpec(memory_space=pl.ANY)] * 2,
        out_specs=pl.BlockSpec(memory_space=pltpu.VMEM),
        scratch_shapes=[
            pltpu.VMEM((6, TOK, DIM), jnp.bfloat16),
            pltpu.VMEM((6, TAG_ROWS, LANES), jnp.int32),
            pltpu.VMEM((6, TOK, LANES), jnp.float32),
            pltpu.VMEM((6, TOK, LANES), jnp.float32),
            pltpu.VMEM((4, 8, TOK), jnp.float32),
            pltpu.VMEM((6, TAG_ROWS, LANES), jnp.float32),
            pltpu.VMEM((4, TAG_ROWS, LANES), jnp.float32),
            dma((2,)),
            dma((Y_PIECES,)), dma((Y_PIECES,)),
            dma, dma,
            dma((Y_PIECES,)), dma((Y_PIECES,)),
            dma, dma,
            *pair, *pair, *pair, *pair,
            dma((Z_PIECES,)), dma((Z_PIECES,)),
            dma((Z_PIECES,)), dma((Z_PIECES,)),
            *pair, *pair,
            dma((5,)), dma((4,)),
        ],
        compiler_params=pltpu.CompilerParams(collective_id=0, has_side_effects=True),
        name="window",
    )(vectors, docs.reshape(TAG_ROWS, LANES))
    return jnp.maximum(prior, found.reshape(TOK))


def solution(mesh):
    return jax.shard_map(
        per_device,
        mesh=mesh,
        in_specs=(P(("slab", "corpus"), None), P(("slab", "corpus")), P(("slab", "corpus"))),
        out_specs=P(("slab", "corpus")),
        check_vma=False,
    )
```

```python
import jax
import jax.numpy as jnp
from jax import lax
from jax.experimental import pallas as pl
from jax.experimental.pallas import tpu as pltpu
from jax.sharding import PartitionSpec as P

MESH = pl.DeviceIdType.MESH
NEG = -1e30
TOK = 2048
HALF = TOK // 2
DIM = 128
LANES = 128
TAG_ROWS = TOK // LANES
HALF_TAGS = TAG_ROWS // 2
Z_PIECES = 4
Z_ROWS = HALF // Z_PIECES
Y_PIECES = 4
B_AFTER = 1
Y_ROWS = TOK // Y_PIECES
BODY = 512
WIDTH = 512
DIRECT, RELAYED, GROUP = 0, HALF, TOK
BLOCK_ROWS = TOK + 8 * TOK
LEFT_ROWS = TOK + 4 * TOK


def scope(name):
    return jax.named_scope(name)


def kernel(
    v_ref, d_ref, o_ref,
    buf, tags, wide, rows, cols, res, ret,
    own_sem, a_send, a_recv, c_send, c_recv, b_send, b_recv, f_send, f_recv, z_send, z_recv, r_send, r_recv,
    t_send, t_recv, m_send, m_recv,
):
    slab, corpus = lax.axis_index("slab"), lax.axis_index("corpus")
    x, zh, y = corpus // 8, (corpus // 4) % 2, corpus % 4
    core = slab % 2
    takes = (zh + core) % 2 == 1
    gives = (zh + core) % 2 == 0
    half = (zh + core + 1) % 2
    partner = slab + 1 - 2 * core
    other = 1 - zh
    dx = 1 - 2 * zh

    def place(px, pz, py, s=slab):
        return (s, ((px + 4) % 4) * 8 + pz * 4 + (py + 4) % 4)

    def block(b):
        return pl.multiple_of(GROUP + b * TOK, TOK)

    def remote(src, dst, send, recv, to):
        return pltpu.make_async_remote_copy(
            src_ref=src, dst_ref=dst, send_sem=send, recv_sem=recv, device_id=to, device_id_type=MESH
        )

    def at(start, count):
        return buf.at[pl.ds(pl.multiple_of(start, 16), count)]

    def tag_at(start, count):
        return tags.at[pl.ds(pl.multiple_of(start, 8), count)]

    def tag_row(row):
        return row // LANES

    up, two, down = (y + 1) % 4, (y + 2) % 4, (y + 3) % 4
    near = jnp.where(takes, up, down)
    ahead = place(x, zh, jnp.where(takes, y - 1, y + 1))
    group = jnp.where(takes, 0, 4)
    own_row, near_row, two_row = block(y), block(near), block(two)

    barrier = pltpu.get_barrier_semaphore()

    def hello(ids):
        for to in ids:
            pl.semaphore_signal(barrier, inc=1, device_id=to, device_id_type=MESH)
        pl.semaphore_wait(barrier, len(ids))

    mates = [place(x, zh, y + k) for k in (1, 2, 3)]
    cross = [place(x, zh, y + k, partner) for k in (0, 1, 2, 3)]
    sides = [place(x + 1, zh, y), place(x - 1, zh, y)]
    far = [place(x, other, y), place(x - dx, other, y)]
    far_partner = [place(x, other, y, partner), place(x - dx, other, y, partner)]

    def a_copy(c):
        return remote(
            v_ref.at[pl.ds(c * Y_ROWS, Y_ROWS)], at(own_row + c * Y_ROWS, Y_ROWS), a_send.at[c], a_recv.at[c], ahead
        )

    def c_copy(c):
        spot = at(near_row + c * Y_ROWS, Y_ROWS)
        return remote(spot, spot, c_send.at[c], c_recv.at[c], ahead)

    b_copy = remote(v_ref, at(own_row, TOK), b_send, b_recv, mates[0])

    def z_copy(h, j):
        return remote(
            v_ref.at[pl.ds(h * HALF + j * Z_ROWS, Z_ROWS)], at(DIRECT + j * Z_ROWS, Z_ROWS),
            z_send.at[h * Z_PIECES + j], z_recv.at[j], (far if h == 0 else far_partner)[0],
        )

    def r_copy(j):
        return remote(
            at(DIRECT + j * Z_ROWS, Z_ROWS), at(RELAYED + j * Z_ROWS, Z_ROWS), r_send.at[j], r_recv.at[j],
            place(x + dx, zh, y),
        )

    def forward(k):
        src = v_ref if k == 0 else at(block((y + k) % 4), TOK)
        return remote(src, at(block(4 + (y + k) % 4), TOK), f_send.at[k], f_recv.at[k], cross[0])

    def tag_copy(k):
        own_tags, near_tags = tag_row(own_row), tag_row(near_row)
        src, dst, to = [
            (d_ref, tag_at(own_tags, TAG_ROWS), ahead),
            (tag_at(near_tags, TAG_ROWS), tag_at(near_tags, TAG_ROWS), ahead),
            (d_ref, tag_at(own_tags, TAG_ROWS), mates[0]),
            (d_ref.at[pl.ds(0, HALF_TAGS)], tag_at(0, HALF_TAGS), far[0]),
            (d_ref.at[pl.ds(HALF_TAGS, HALF_TAGS)], tag_at(0, HALF_TAGS), far_partner[0]),
            (tag_at(0, HALF_TAGS), tag_at(HALF_TAGS, HALF_TAGS), place(x + dx, zh, y)),
        ][k]
        return remote(src, dst, t_send.at[k], t_recv.at[min(k, 3) if k < 5 else 4], to)

    def tag_forward(k):
        src = d_ref if k == 0 else tag_at(tag_row(block((y + k) % 4)), TAG_ROWS)
        return remote(src, tag_at(tag_row(block(4 + (y + k) % 4)), TAG_ROWS), t_send.at[6 + k], t_recv.at[5 + k], cross[0])

    own_v = pltpu.make_async_copy(v_ref, at(own_row, TOK), own_sem.at[0])
    own_d = pltpu.make_async_copy(d_ref, tag_at(tag_row(own_row), TAG_ROWS), own_sem.at[1])

    def widen(row, count):
        shape = (LANES, LANES)
        eye = lax.broadcasted_iota(jnp.int32, shape, 0) == lax.broadcasted_iota(jnp.int32, shape, 1)
        labels = tags[pl.ds(pl.multiple_of(tag_row(row), 8), count // LANES), :].astype(jnp.float32)
        spread = jnp.concatenate(
            [
                jnp.where(eye, jnp.broadcast_to(labels[q : q + 1, :], shape), 0.0).astype(jnp.bfloat16)
                for q in range(count // LANES)
            ],
            axis=0,
        )
        wide[pl.ds(pl.multiple_of(row, LANES), count), :] = jnp.dot(
            spread, jnp.ones(shape, jnp.bfloat16), preferred_element_type=jnp.float32
        )

    def tile(left, right, first, body=BODY):
        spot = pl.ds(pl.multiple_of(left, BODY), body)
        labels = tags[pl.ds(pl.multiple_of(tag_row(right), 8), TAG_ROWS), :].astype(jnp.float32)
        b = (right - GROUP) // TOK
        for w in range(TOK // WIDTH):
            scores = lax.dot_general(
                buf[spot, :], buf[pl.ds(pl.multiple_of(right + w * WIDTH, WIDTH), WIDTH), :],
                (((1,), (1,)), ((), ())), preferred_element_type=jnp.float32,
            )
            marks = wide[spot, :]
            best = None if first and w == 0 else rows[spot, :]
            for k in range(WIDTH // LANES):
                q = w * (WIDTH // LANES) + k
                part = jnp.where(marks == labels[q : q + 1, :], NEG, scores[:, k * LANES : (k + 1) * LANES])
                best = part if best is None else jnp.maximum(best, part)
                peak = jnp.max(part.reshape(body // 8, 8, LANES), axis=0)
                lanes = slice(q * LANES, (q + 1) * LANES)
                cols[b, :, lanes] = jnp.maximum(cols[b, :, lanes], peak)
            rows[spot, :] = best

    def row_peaks(row, count):
        part = rows[pl.ds(pl.multiple_of(row, LANES), count), :]
        return jnp.max(part.reshape(count // LANES, LANES, LANES), axis=2)

    def col_peaks(b):
        return jnp.concatenate(
            [jnp.max(cols[b, :, q * LANES : (q + 1) * LANES], axis=0, keepdims=True) for q in range(TAG_ROWS)], axis=0
        )

    def message(src, count, dst, send, recv, to):
        slot, start = dst
        return remote(
            res.at[pl.ds(pl.multiple_of(src, 8), count)], ret.at[slot, pl.ds(start, count)],
            m_send.at[send], m_recv.at[recv], to,
        )

    def res_row(b):
        return pl.multiple_of(tag_row(block(b)), TAG_ROWS)

    late = jnp.where(y < 2, two, y)
    early = jnp.where(y < 2, y, two)
    late_row = block(late) + jnp.where(y < 2, 0, HALF)
    minus = jnp.where(zh == 1, DIRECT, RELAYED)
    plus = jnp.where(zh == 1, RELAYED, DIRECT)
    center = block(group + y)

    own_v.start()
    own_d.start()

    with scope("hello"):
        @pl.when(takes)
        def _():
            hello(mates + cross + sides + far)
            tag_forward(0).start()
            forward(0).start()
            tag_copy(0).start()
            for c in range(Y_PIECES):
                a_copy(c).start()

        @pl.when(gives)
        def _():
            hello(mates + cross + sides + far + far_partner)
            tag_copy(3).start()
            tag_copy(4).start()
            for j in range(Z_PIECES):
                z_copy(0, j).start()
                z_copy(1, j).start()
            tag_copy(0).start()
            for c in range(Y_PIECES):
                a_copy(c).start()

    with scope("init"):
        cols[...] = jnp.full(cols.shape, NEG, jnp.float32)
        res[...] = jnp.full(res.shape, NEG, jnp.float32)
        own_v.wait()
        own_d.wait()
        widen(own_row, TOK)

    def pass_on(c, do):
        if c < Y_PIECES // 2:
            getattr(c_copy(c), do)()
        else:
            whole = takes | ((y >= 2) if do == "wait_recv" else (y == 1) | (y == 2))

            @pl.when(whole)
            def _():
                getattr(c_copy(c), do)()

    def on_near(c):
        with scope("near%d" % c):
            if c == 0:
                tag_copy(0).wait_recv()
                tag_copy(1).start()
                widen(near_row, TOK)
            a_copy(c).wait_recv()

            @pl.when(takes)
            def _():
                c_copy(c).start()

            if c == B_AFTER:
                @pl.when(takes)
                def _():
                    tag_copy(2).start()
                    b_copy.start()

            if c == Y_PIECES - 1:
                @pl.when(takes)
                def _():
                    tag_forward(1).start()
                    forward(1).start()

                @pl.when(gives)
                def _():
                    for k in range(Y_PIECES):
                        pass_on(k, "start")
            tile(near_row + c * Y_ROWS, own_row, True)

    def on_z(j):
        with scope("z%d" % j):
            if j == 0:
                tag_copy(3).wait_recv()
                tag_copy(5).start()
            z_copy(0, j).wait_recv()
            r_copy(j).start()

    def on_direct(i):
        with scope("dir%d" % i):
            if i == 0:
                @pl.when(gives)
                def _():
                    tag_forward(0).wait_recv()
                    forward(0).wait_recv()
                widen(DIRECT, HALF)
            tile(DIRECT + i * BODY, center, True)

    def on_two():
        with scope("two"):
            @pl.when(takes)
            def _():
                tag_copy(1).wait_recv()
                for c in range(Y_PIECES):
                    c_copy(c).wait_recv()
                tag_forward(2).start()
                forward(2).start()

    def on_down():
        with scope("down"):
            @pl.when(takes)
            def _():
                tag_copy(2).wait_recv()
                b_copy.wait_recv()
                tag_forward(3).start()
                forward(3).start()

    def others(i, ks):
        for k in ks:
            if i == 0:
                @pl.when(gives)
                def _():
                    tag_forward(k).wait_recv()
                    forward(k).wait_recv()

            b = (y + k) % 4
            tile(jnp.where(b > y, plus, minus) + i * BODY, block(group + b), False)

    def on_relayed(i):
        if i == 0:
            tag_copy(5).wait_recv()
            widen(RELAYED, HALF)
        r_copy(2 * i).wait_recv()
        r_copy(2 * i + 1).wait_recv()
        tile(RELAYED + i * BODY, center, True)

    on_near(0)
    on_near(1)
    on_z(0)
    on_near(2)
    on_z(1)
    on_near(3)
    on_direct(0)
    on_z(2)
    with scope("rel0"):
        on_relayed(0)
    with scope("oth0a"):
        others(0, (1,))
    on_two()
    on_z(3)
    with scope("oth0b"):
        others(0, (2,))
    on_direct(1)
    on_down()
    with scope("oth0c"):
        others(0, (3,))
    with scope("rel1"):
        on_relayed(1)
    with scope("oth1"):
        others(1, (1, 2, 3))

    with scope("zpeaks"):
        res[0:TAG_ROWS, :] = row_peaks(0, TOK)

        @pl.when(takes)
        def _():
            message(0, HALF_TAGS, (0, 0), 0, 0, far[0]).start()
            message(HALF_TAGS, HALF_TAGS, (1, 0), 1, 2, far[1]).start()

        @pl.when(gives)
        def _():
            message(0, HALF_TAGS, (0, HALF_TAGS), 0, 1, far_partner[0]).start()
            message(HALF_TAGS, HALF_TAGS, (1, HALF_TAGS), 1, 3, far_partner[1]).start()
            for k in (1, 2, 3, 0):
                b = 4 + (y + k) % 4
                slot = 3 + (4 - k) % 4
                res[pl.ds(res_row(b), TAG_ROWS), :] = col_peaks(b)
                message(res_row(b), TAG_ROWS, (slot, 0), 4 + k, slot, cross[k]).start()

    with scope("opp"):
        @pl.when(gives)
        def _():
            tag_copy(1).wait_recv()
            for c in range(Y_PIECES):
                pass_on(c, "wait_recv")

        widen(two_row, TOK)
        tile(late_row, block(early), True)
        tile(late_row + BODY, block(early), True)

    with scope("peaks"):
        res[pl.ds(res_row(near), TAG_ROWS), :] = row_peaks(near_row, TOK)
        res[pl.ds(pl.multiple_of(tag_row(late_row), HALF_TAGS), HALF_TAGS), :] = row_peaks(late_row, HALF)
        for k in (2, 1, 3, 0):
            b = (y + k) % 4
            spot = pl.ds(res_row(b), TAG_ROWS)
            res[spot, :] = jnp.maximum(res[spot, :], col_peaks(b))

            @pl.when(takes)
            def _():
                if k:
                    message(res_row(b), TAG_ROWS, (3 - k, 0), 1 + k, 3 - k, mates[k - 1]).start()

            @pl.when(gives)
            def _():
                if k == 3:
                    message(res_row(b), TAG_ROWS, (2, 0), 2, 4, mates[2]).start()
                if k == 2:
                    message(res_row(b), TAG_ROWS, (3, 0), 3, 5, mates[1]).start()

    with scope("final"):
        @pl.when(takes)
        def _():
            best = res[pl.ds(res_row(y), TAG_ROWS), :]
            for slot in range(7):
                message(0, TAG_ROWS, (slot, 0), 0, slot, mates[0]).wait_recv()
                best = jnp.maximum(best, ret[slot])
            o_ref[...] = best

        @pl.when(gives)
        def _():
            best = res[pl.ds(res_row(y), TAG_ROWS), :]
            for slot in (2, 3):
                message(0, TAG_ROWS, (slot, 0), 0, slot + 2, mates[0]).wait_recv()
                best = jnp.maximum(best, ret[slot])
            for sem in range(4):
                message(0, HALF_TAGS, (0, 0), 0, sem, mates[0]).wait_recv()
            for slot in (0, 1):
                best = jnp.maximum(best, ret[slot])
            o_ref[...] = best

    with scope("drain"):
        for c in range(Y_PIECES):
            a_copy(c).wait_send()
            pass_on(c, "wait_send")
        for j in range(Z_PIECES):
            r_copy(j).wait_send()
        for k in (0, 1, 5):
            tag_copy(k).wait_send()

        @pl.when(takes)
        def _():
            b_copy.wait_send()
            tag_copy(2).wait_send()
            for k in range(4):
                forward(k).wait_send()
                tag_forward(k).wait_send()
            for sem in range(5):
                message(0, HALF_TAGS if sem < 2 else TAG_ROWS, (0, 0), sem, 0, mates[0]).wait_send()

        @pl.when(gives)
        def _():
            for j in range(Z_PIECES):
                z_copy(0, j).wait_send()
                z_copy(1, j).wait_send()
            tag_copy(3).wait_send()
            tag_copy(4).wait_send()
            for sem in range(8):
                message(0, HALF_TAGS if sem < 2 else TAG_ROWS, (0, 0), sem, 0, mates[0]).wait_send()


def per_device(vectors, docs, prior):
    dma = pltpu.SemaphoreType.DMA
    found = pl.pallas_call(
        kernel,
        out_shape=jax.ShapeDtypeStruct((TAG_ROWS, LANES), jnp.float32),
        in_specs=[pl.BlockSpec(memory_space=pl.ANY)] * 2,
        out_specs=pl.BlockSpec(memory_space=pltpu.VMEM),
        scratch_shapes=[
            pltpu.VMEM((BLOCK_ROWS, DIM), jnp.bfloat16),
            pltpu.VMEM((BLOCK_ROWS // LANES, LANES), jnp.int32),
            pltpu.VMEM((LEFT_ROWS, LANES), jnp.float32),
            pltpu.VMEM((LEFT_ROWS, LANES), jnp.float32),
            pltpu.VMEM((8, 8, TOK), jnp.float32),
            pltpu.VMEM((BLOCK_ROWS // LANES, LANES), jnp.float32),
            pltpu.VMEM((7, TAG_ROWS, LANES), jnp.float32),
            dma((2,)),
            dma((Y_PIECES,)), dma((Y_PIECES,)),
            dma((Y_PIECES,)), dma((Y_PIECES,)),
            dma, dma,
            dma((4,)), dma((4,)),
            dma((2 * Z_PIECES,)), dma((Z_PIECES,)),
            dma((Z_PIECES,)), dma((Z_PIECES,)),
            dma((10,)), dma((9,)),
            dma((8,)), dma((7,)),
        ],
        compiler_params=pltpu.CompilerParams(collective_id=0, has_side_effects=True),
        name="window",
    )(vectors, docs.reshape(TAG_ROWS, LANES))
    return jnp.maximum(prior, found.reshape(TOK))


def solution(mesh):
    return jax.shard_map(
        per_device,
        mesh=mesh,
        in_specs=(P(("slab", "corpus"), None), P(("slab", "corpus")), P(("slab", "corpus"))),
        out_specs=P(("slab", "corpus")),
        check_vma=False,
    )
```

```python
import jax
import jax.numpy as jnp
from jax import lax
from jax.experimental import pallas as pl
from jax.experimental.pallas import tpu as pltpu
from jax.sharding import PartitionSpec as P

MESH = pl.DeviceIdType.MESH
NEG = -1e30
TOK = 2048
HALF = TOK // 2
DIM = 128
LANES = 128
TAG_ROWS = TOK // LANES
HALF_TAGS = TAG_ROWS // 2
Z_PIECES = 4
Z_ROWS = HALF // Z_PIECES
Y_PIECES = 4
Y_ROWS = TOK // Y_PIECES
BODY = 512
GROUPS = ((0, 512), (512, 256), (768, 256))
WIDTH = 512
DIRECT, RELAYED, GROUP = 0, HALF, TOK
BLOCK_ROWS = TOK + 8 * TOK
LEFT_ROWS = TOK + 4 * TOK


def scope(name):
    return jax.named_scope(name)


def kernel(
    v_ref, d_ref, o_ref,
    buf, tags, wide, rows, cols, res, ret,
    own_sem, a_send, a_recv, c_send, c_recv, b_send, b_recv, f_send, f_recv, z_send, z_recv, r_send, r_recv,
    t_send, t_recv, m_send, m_recv,
):
    slab, corpus = lax.axis_index("slab"), lax.axis_index("corpus")
    x, zh, y = corpus // 8, (corpus // 4) % 2, corpus % 4
    core = slab % 2
    takes = (zh + core) % 2 == 1
    gives = (zh + core) % 2 == 0
    half = (zh + core + 1) % 2
    partner = slab + 1 - 2 * core
    other = 1 - zh
    dx = 1 - 2 * zh

    def place(px, pz, py, s=slab):
        return (s, ((px + 4) % 4) * 8 + pz * 4 + (py + 4) % 4)

    def block(b):
        return pl.multiple_of(GROUP + b * TOK, TOK)

    def remote(src, dst, send, recv, to):
        return pltpu.make_async_remote_copy(
            src_ref=src, dst_ref=dst, send_sem=send, recv_sem=recv, device_id=to, device_id_type=MESH
        )

    def at(start, count):
        return buf.at[pl.ds(pl.multiple_of(start, 16), count)]

    def tag_at(start, count):
        return tags.at[pl.ds(pl.multiple_of(start, 8), count)]

    def tag_row(row):
        return row // LANES

    up, two, down = (y + 1) % 4, (y + 2) % 4, (y + 3) % 4
    near = jnp.where(takes, up, down)
    ahead = place(x, zh, jnp.where(takes, y - 1, y + 1))
    group = jnp.where(takes, 0, 4)
    own_row, near_row, two_row = block(y), block(near), block(two)

    barrier = pltpu.get_barrier_semaphore()

    def hello(greeted, awaited):
        for to in greeted:
            pl.semaphore_signal(barrier, inc=1, device_id=to, device_id_type=MESH)
        pl.semaphore_wait(barrier, awaited)

    mates = [place(x, zh, y + k) for k in (1, 2, 3)]
    cross = [place(x, zh, y + k, partner) for k in (0, 1, 2, 3)]
    feeder = place(x - dx, zh, y)
    far = [place(x, other, y), place(x - dx, other, y)]
    far_partner = [place(x, other, y, partner), place(x - dx, other, y, partner)]

    def a_copy(c):
        return remote(
            v_ref.at[pl.ds(c * Y_ROWS, Y_ROWS)], at(own_row + c * Y_ROWS, Y_ROWS), a_send.at[c], a_recv.at[c], ahead
        )

    def c_copy(c):
        spot = at(near_row + c * Y_ROWS, Y_ROWS)
        return remote(spot, spot, c_send.at[c], c_recv.at[c], ahead)

    def b_copy(c):
        return remote(
            v_ref.at[pl.ds(c * Y_ROWS, Y_ROWS)], at(own_row + c * Y_ROWS, Y_ROWS), b_send.at[c], b_recv.at[c], mates[0]
        )


    def z_copy(h, j):
        return remote(
            v_ref.at[pl.ds(h * HALF + j * Z_ROWS, Z_ROWS)], at(DIRECT + j * Z_ROWS, Z_ROWS),
            z_send.at[h * Z_PIECES + j], z_recv.at[j], (far if h == 0 else far_partner)[0],
        )

    def r_copy(j):
        return remote(
            at(DIRECT + j * Z_ROWS, Z_ROWS), at(RELAYED + j * Z_ROWS, Z_ROWS), r_send.at[j], r_recv.at[j],
            place(x + dx, zh, y),
        )

    def forward(k):
        src = v_ref if k == 0 else at(block((y + k) % 4), TOK)
        return remote(src, at(block(4 + (y + k) % 4), TOK), f_send.at[k], f_recv.at[k], cross[0])

    def tag_copy(k):
        own_tags, near_tags = tag_row(own_row), tag_row(near_row)
        src, dst, to = [
            (d_ref, tag_at(own_tags, TAG_ROWS), ahead),
            (tag_at(near_tags, TAG_ROWS), tag_at(near_tags, TAG_ROWS), ahead),
            (d_ref, tag_at(own_tags, TAG_ROWS), mates[0]),
            (d_ref.at[pl.ds(0, HALF_TAGS)], tag_at(0, HALF_TAGS), far[0]),
            (d_ref.at[pl.ds(HALF_TAGS, HALF_TAGS)], tag_at(0, HALF_TAGS), far_partner[0]),
            (tag_at(0, HALF_TAGS), tag_at(HALF_TAGS, HALF_TAGS), place(x + dx, zh, y)),
        ][k]
        return remote(src, dst, t_send.at[k], t_recv.at[min(k, 3) if k < 5 else 4], to)

    def tag_forward(k):
        src = d_ref if k == 0 else tag_at(tag_row(block((y + k) % 4)), TAG_ROWS)
        return remote(src, tag_at(tag_row(block(4 + (y + k) % 4)), TAG_ROWS), t_send.at[6 + k], t_recv.at[5 + k], cross[0])

    own_v = pltpu.make_async_copy(v_ref, at(own_row, TOK), own_sem.at[0])
    own_d = pltpu.make_async_copy(d_ref, tag_at(tag_row(own_row), TAG_ROWS), own_sem.at[1])

    def widen(row, count):
        shape = (LANES, LANES)
        eye = lax.broadcasted_iota(jnp.int32, shape, 0) == lax.broadcasted_iota(jnp.int32, shape, 1)
        labels = tags[pl.ds(pl.multiple_of(tag_row(row), 8), count // LANES), :].astype(jnp.float32)
        spread = jnp.concatenate(
            [
                jnp.where(eye, jnp.broadcast_to(labels[q : q + 1, :], shape), 0.0).astype(jnp.bfloat16)
                for q in range(count // LANES)
            ],
            axis=0,
        )
        wide[pl.ds(pl.multiple_of(row, LANES), count), :] = jnp.dot(
            spread, jnp.ones(shape, jnp.bfloat16), preferred_element_type=jnp.float32
        )

    def tile(left, right, first, body=BODY):
        spot = pl.ds(pl.multiple_of(left, body), body)
        labels = tags[pl.ds(pl.multiple_of(tag_row(right), 8), TAG_ROWS), :].astype(jnp.float32)
        b = (right - GROUP) // TOK
        for w in range(TOK // WIDTH):
            scores = lax.dot_general(
                buf[spot, :], buf[pl.ds(pl.multiple_of(right + w * WIDTH, WIDTH), WIDTH), :],
                (((1,), (1,)), ((), ())), preferred_element_type=jnp.float32,
            )
            marks = wide[spot, :]
            best = None if first and w == 0 else rows[spot, :]
            for k in range(WIDTH // LANES):
                q = w * (WIDTH // LANES) + k
                part = jnp.where(marks == labels[q : q + 1, :], NEG, scores[:, k * LANES : (k + 1) * LANES])
                best = part if best is None else jnp.maximum(best, part)
                peak = jnp.max(part.reshape(body // 8, 8, LANES), axis=0)
                lanes = slice(q * LANES, (q + 1) * LANES)
                cols[b, :, lanes] = jnp.maximum(cols[b, :, lanes], peak)
            rows[spot, :] = best

    def row_peaks(row, count):
        part = rows[pl.ds(pl.multiple_of(row, LANES), count), :]
        return jnp.max(part.reshape(count // LANES, LANES, LANES), axis=2)

    def col_peaks(b):
        return jnp.concatenate(
            [jnp.max(cols[b, :, q * LANES : (q + 1) * LANES], axis=0, keepdims=True) for q in range(TAG_ROWS)], axis=0
        )

    def message(src, count, dst, send, recv, to):
        slot, start = dst
        return remote(
            res.at[pl.ds(pl.multiple_of(src, 8), count)], ret.at[slot, pl.ds(start, count)],
            m_send.at[send], m_recv.at[recv], to,
        )

    def res_row(b):
        return pl.multiple_of(tag_row(block(b)), TAG_ROWS)

    late = jnp.where(y < 2, two, y)
    early = jnp.where(y < 2, y, two)
    late_row = block(late) + jnp.where(y < 2, 0, HALF)
    minus = jnp.where(zh == 1, DIRECT, RELAYED)
    plus = jnp.where(zh == 1, RELAYED, DIRECT)
    center = block(group + y)

    def start_b(c):
        if c == 0:
            tag_copy(2).start()
        b_copy(c).start()

    own_v.start()
    own_d.start()

    with scope("hello"):
        @pl.when(takes)
        def _():
            hello([far[0], feeder, *mates, *cross], 5)
            tag_copy(0).start()
            for c in range(Y_PIECES):
                a_copy(c).start()
            tag_forward(0).start()
            forward(0).start()

            @pl.when(zh == 0)
            def _():
                for c in range(Y_PIECES):
                    start_b(c)

        @pl.when(gives)
        def _():
            hello([far_partner[0], feeder, *mates, cross[0]], 10)
            tag_copy(3).start()
            tag_copy(4).start()
            for j in range(Z_PIECES):
                z_copy(0, j).start()
                z_copy(1, j).start()
            tag_copy(0).start()
            for c in range(Y_PIECES):
                a_copy(c).start()

    with scope("init"):
        cols[...] = jnp.full(cols.shape, NEG, jnp.float32)
        res[...] = jnp.full(res.shape, NEG, jnp.float32)
        own_v.wait()
        own_d.wait()
        widen(own_row, TOK)

    def pass_on(c, do):
        if c < Y_PIECES // 2:
            getattr(c_copy(c), do)()
        else:
            whole = takes | ((y >= 2) if do == "wait_recv" else (y == 1) | (y == 2))

            @pl.when(whole)
            def _():
                getattr(c_copy(c), do)()

    def on_near(c):
        with scope("near%d" % c):
            if c == 0:
                tag_copy(0).wait_recv()
                widen(near_row, TOK)
            a_copy(c).wait_recv()
            tile(near_row + c * Y_ROWS, own_row, True)

    def on_receiver_near(c):
        a_copy(c).wait_recv()
        c_copy(c).start()
        if c == Y_PIECES - 1:
            tag_forward(1).start()
            forward(1).start()

        @pl.when(zh == 1)
        def _():
            start_b(c)

        tile(near_row + c * Y_ROWS, own_row, True)

    def on_z(j):
        with scope("z%d" % j):
            if j == 0:
                tag_copy(3).wait_recv()
                tag_copy(5).start()
            z_copy(0, j).wait_recv()
            r_copy(j).start()

    def on_direct(i):
        with scope("dir%d" % i):
            if i == 0:
                @pl.when(gives)
                def _():
                    tag_forward(0).wait_recv()
                    forward(0).wait_recv()
                tag_copy(5).wait_recv()
                widen(DIRECT, TOK)
            start, count = GROUPS[i]
            tile(DIRECT + start, center, True, count)

    def on_two():
        with scope("two"):
            @pl.when(takes)
            def _():
                tag_copy(1).wait_recv()
                for c in range(Y_PIECES):
                    c_copy(c).wait_recv()
                tag_forward(2).start()
                forward(2).start()

    def on_down():
        with scope("down"):
            @pl.when(takes)
            def _():
                tag_copy(2).wait_recv()
                for c in range(Y_PIECES):
                    b_copy(c).wait_recv()
                tag_forward(3).start()
                forward(3).start()

    def others(i, ks):
        start, count = GROUPS[i]
        for k in ks:
            if i == 0:
                @pl.when(gives)
                def _():
                    tag_forward(k).wait_recv()
                    forward(k).wait_recv()

            b = (y + k) % 4
            tile(jnp.where(b > y, plus, minus) + start, block(group + b), False, count)

    def on_relayed(i):
        start, count = GROUPS[i]
        for j in range(start // Z_ROWS, (start + count) // Z_ROWS):
            r_copy(j).wait_recv()
        tile(RELAYED + start, center, True, count)

    @pl.when(takes)
    def _():
        with scope("recv01"):
            tag_copy(0).wait_recv()
            tag_copy(1).start()
            widen(near_row, TOK)
            on_receiver_near(0)
            on_receiver_near(1)

    on_z(0)

    @pl.when(takes)
    def _():
        with scope("recv23"):
            on_receiver_near(2)
            on_receiver_near(3)

    @pl.when(gives)
    def _():
        on_near(0)
        on_near(1)

    on_z(1)
    on_direct(0)

    @pl.when(gives)
    def _():
        tag_copy(1).start()
        pass_on(0, "start")
        pass_on(1, "start")
        for c in (2, 3):
            with scope("near%d" % c):
                a_copy(c).wait_recv()
                pass_on(c, "start")
                tile(near_row + c * Y_ROWS, own_row, True)

    on_z(2)

    @pl.when(gives)
    def _():
        with scope("adj"):
            res[pl.ds(res_row(near), TAG_ROWS), :] = row_peaks(near_row, TOK)
            message(res_row(near), TAG_ROWS, (2, 0), 2, 4, mates[2]).start()

    on_two()
    on_down()
    on_direct(1)
    with scope("rel0"):
        on_relayed(0)
    with scope("oth0a"):
        others(0, (1,))
    on_z(3)
    with scope("oth0b"):
        others(0, (2,))

    with scope("oth0c"):
        others(0, (3,))
    with scope("rel1"):
        on_relayed(1)
    with scope("oth1"):
        others(1, (1, 2, 3))
    on_direct(2)
    with scope("rel2"):
        on_relayed(2)
    with scope("oth2"):
        others(2, (1, 2, 3))

    with scope("zpeaks"):
        res[0:TAG_ROWS, :] = row_peaks(0, TOK)

        @pl.when(takes)
        def _():
            message(0, HALF_TAGS, (0, 0), 0, 0, far[0]).start()
            message(HALF_TAGS, HALF_TAGS, (1, 0), 1, 2, far[1]).start()

        @pl.when(gives)
        def _():
            message(0, HALF_TAGS, (0, HALF_TAGS), 0, 1, far_partner[0]).start()
            message(HALF_TAGS, HALF_TAGS, (1, HALF_TAGS), 1, 3, far_partner[1]).start()
            for k in (1, 2, 3, 0):
                b = 4 + (y + k) % 4
                slot = 3 + (4 - k) % 4
                res[pl.ds(res_row(b), TAG_ROWS), :] = col_peaks(b)
                message(res_row(b), TAG_ROWS, (slot, 0), 4 + k, slot, cross[k]).start()

    def settle(k):
        spot = pl.ds(res_row((y + k) % 4), TAG_ROWS)
        res[spot, :] = jnp.maximum(res[spot, :], col_peaks((y + k) % 4))

    def to_mate(k):
        settle(k)
        message(res_row((y + k) % 4), TAG_ROWS, (3 - k, 0), 1 + k, 3 - k, mates[k - 1]).start()

    @pl.when(takes)
    def _():
        with scope("rpeaks"):
            res[pl.ds(res_row(near), TAG_ROWS), :] = row_peaks(near_row, TOK)
            to_mate(1)
            to_mate(3)

    with scope("opp"):
        @pl.when(gives)
        def _():
            tag_copy(1).wait_recv()
            for c in range(Y_PIECES):
                pass_on(c, "wait_recv")

        widen(two_row, TOK)
        tile(late_row, block(early), True)
        tile(late_row + BODY, block(early), True)

    with scope("peaks"):
        res[pl.ds(pl.multiple_of(tag_row(late_row), HALF_TAGS), HALF_TAGS), :] = row_peaks(late_row, HALF)

        @pl.when(takes)
        def _():
            to_mate(2)

        @pl.when(gives)
        def _():
            settle(2)
            message(res_row(two), TAG_ROWS, (3, 0), 3, 5, mates[1]).start()

        settle(0)

    with scope("final"):
        @pl.when(takes)
        def _():
            best = res[pl.ds(res_row(y), TAG_ROWS), :]
            for slot in range(7):
                message(0, TAG_ROWS, (slot, 0), 0, slot, mates[0]).wait_recv()
                best = jnp.maximum(best, ret[slot])
            o_ref[...] = best

        @pl.when(gives)
        def _():
            best = res[pl.ds(res_row(y), TAG_ROWS), :]
            for slot in (2, 3):
                message(0, TAG_ROWS, (slot, 0), 0, slot + 2, mates[0]).wait_recv()
                best = jnp.maximum(best, ret[slot])
            for sem in range(4):
                message(0, HALF_TAGS, (0, 0), 0, sem, mates[0]).wait_recv()
            for slot in (0, 1):
                best = jnp.maximum(best, ret[slot])
            o_ref[...] = best

    with scope("drain"):
        for c in range(Y_PIECES):
            a_copy(c).wait_send()
            pass_on(c, "wait_send")
        for j in range(Z_PIECES):
            r_copy(j).wait_send()
        for k in (0, 1, 5):
            tag_copy(k).wait_send()

        @pl.when(takes)
        def _():
            for c in range(Y_PIECES):
                b_copy(c).wait_send()
            tag_copy(2).wait_send()
            for k in range(4):
                forward(k).wait_send()
                tag_forward(k).wait_send()
            for sem in range(5):
                message(0, HALF_TAGS if sem < 2 else TAG_ROWS, (0, 0), sem, 0, mates[0]).wait_send()

        @pl.when(gives)
        def _():
            for j in range(Z_PIECES):
                z_copy(0, j).wait_send()
                z_copy(1, j).wait_send()
            tag_copy(3).wait_send()
            tag_copy(4).wait_send()
            for sem in range(8):
                message(0, HALF_TAGS if sem < 2 else TAG_ROWS, (0, 0), sem, 0, mates[0]).wait_send()


def per_device(vectors, docs, prior):
    dma = pltpu.SemaphoreType.DMA
    found = pl.pallas_call(
        kernel,
        out_shape=pltpu.VMEM((TAG_ROWS, LANES), jnp.float32),
        in_specs=[pl.BlockSpec(memory_space=pl.ANY)] * 2,
        out_specs=pl.BlockSpec(memory_space=pltpu.VMEM),
        scratch_shapes=[
            pltpu.VMEM((BLOCK_ROWS, DIM), jnp.bfloat16),
            pltpu.VMEM((BLOCK_ROWS // LANES, LANES), jnp.int32),
            pltpu.VMEM((LEFT_ROWS, LANES), jnp.float32),
            pltpu.VMEM((LEFT_ROWS, LANES), jnp.float32),
            pltpu.VMEM((8, 8, TOK), jnp.float32),
            pltpu.VMEM((BLOCK_ROWS // LANES, LANES), jnp.float32),
            pltpu.VMEM((7, TAG_ROWS, LANES), jnp.float32),
            dma((2,)),
            dma((Y_PIECES,)), dma((Y_PIECES,)),
            dma((Y_PIECES,)), dma((Y_PIECES,)),
            dma((Y_PIECES,)), dma((Y_PIECES,)),
            dma((4,)), dma((4,)),
            dma((2 * Z_PIECES,)), dma((Z_PIECES,)),
            dma((Z_PIECES,)), dma((Z_PIECES,)),
            dma((10,)), dma((9,)),
            dma((8,)), dma((7,)),
        ],
        compiler_params=pltpu.CompilerParams(collective_id=0, has_side_effects=True),
        name="window",
    )(vectors, docs.reshape(TAG_ROWS, LANES))
    return jnp.maximum(prior, found.reshape(TOK))


def solution(mesh):
    return jax.shard_map(
        per_device,
        mesh=mesh,
        in_specs=(P(("slab", "corpus"), None), P(("slab", "corpus")), P(("slab", "corpus"))),
        out_specs=P(("slab", "corpus")),
        check_vma=False,
    )
```

```python
import jax
import jax.numpy as jnp
from jax import lax
from jax.experimental import pallas as pl
from jax.experimental.pallas import tpu as pltpu
from jax.sharding import PartitionSpec as P

MESH = pl.DeviceIdType.MESH
NEG = -1e30
TOK = 2048
HALF = TOK // 2
DIM = 128
LANES = 128
TAG_ROWS = TOK // LANES
HALF_TAGS = TAG_ROWS // 2
Z_PIECES = 8
Z_ROWS = HALF // Z_PIECES
Y_PIECES = 4
Y_ROWS = TOK // Y_PIECES
BODY = 512
GROUPS = ((0, 512), (512, 256), (768, 256))
WIDTH = 512
DIRECT, RELAYED, GROUP = 0, HALF, TOK
BLOCK_ROWS = TOK + 8 * TOK
LEFT_ROWS = TOK + 4 * TOK


def scope(name):
    return jax.named_scope(name)


def kernel(
    v_ref, d_ref, o_ref,
    buf, tags, wide, rows, cols, res, ret,
    own_sem, a_send, a_recv, c_send, c_recv, b_send, b_recv, f_send, f_recv, z_send, z_recv, r_send, r_recv,
    t_send, t_recv, m_send, m_recv,
):
    slab, corpus = lax.axis_index("slab"), lax.axis_index("corpus")
    x, zh, y = corpus // 8, (corpus // 4) % 2, corpus % 4
    core = slab % 2
    takes = (zh + core) % 2 == 1
    gives = (zh + core) % 2 == 0
    half = (zh + core + 1) % 2
    partner = slab + 1 - 2 * core
    other = 1 - zh
    dx = 1 - 2 * zh

    def place(px, pz, py, s=slab):
        return (s, ((px + 4) % 4) * 8 + pz * 4 + (py + 4) % 4)

    def block(b):
        return pl.multiple_of(GROUP + b * TOK, TOK)

    def remote(src, dst, send, recv, to):
        return pltpu.make_async_remote_copy(
            src_ref=src, dst_ref=dst, send_sem=send, recv_sem=recv, device_id=to, device_id_type=MESH
        )

    def at(start, count):
        return buf.at[pl.ds(pl.multiple_of(start, 16), count)]

    def tag_at(start, count):
        return tags.at[pl.ds(pl.multiple_of(start, 8), count)]

    def tag_row(row):
        return row // LANES

    up, two, down = (y + 1) % 4, (y + 2) % 4, (y + 3) % 4
    near = jnp.where(takes, up, down)
    ahead = place(x, zh, jnp.where(takes, y - 1, y + 1))
    group = jnp.where(takes, 0, 4)
    own_row, near_row, two_row = block(y), block(near), block(two)

    barrier = pltpu.get_barrier_semaphore()

    def hello(greeted, awaited):
        for to in greeted:
            pl.semaphore_signal(barrier, inc=1, device_id=to, device_id_type=MESH)
        pl.semaphore_wait(barrier, awaited)

    mates = [place(x, zh, y + k) for k in (1, 2, 3)]
    cross = [place(x, zh, y + k, partner) for k in (0, 1, 2, 3)]
    feeder = place(x - dx, zh, y)
    far = [place(x, other, y), place(x - dx, other, y)]
    far_partner = [place(x, other, y, partner), place(x - dx, other, y, partner)]

    def a_copy(c):
        return remote(
            v_ref.at[pl.ds(c * Y_ROWS, Y_ROWS)], at(own_row + c * Y_ROWS, Y_ROWS), a_send.at[c], a_recv.at[c], ahead
        )

    def c_copy(c):
        spot = at(near_row + c * Y_ROWS, Y_ROWS)
        return remote(spot, spot, c_send.at[c], c_recv.at[c], ahead)

    def b_copy(c):
        return remote(
            v_ref.at[pl.ds(c * Y_ROWS, Y_ROWS)], at(own_row + c * Y_ROWS, Y_ROWS), b_send.at[c], b_recv.at[c], mates[0]
        )


    def z_copy(h, j):
        return remote(
            v_ref.at[pl.ds(h * HALF + j * Z_ROWS, Z_ROWS)], at(DIRECT + j * Z_ROWS, Z_ROWS),
            z_send.at[h * Z_PIECES + j], z_recv.at[j], (far if h == 0 else far_partner)[0],
        )

    def r_copy(j):
        return remote(
            at(DIRECT + j * Z_ROWS, Z_ROWS), at(RELAYED + j * Z_ROWS, Z_ROWS), r_send.at[j], r_recv.at[j],
            place(x + dx, zh, y),
        )

    def forward(k, h=0):
        row, their = block((y + k) % 4), block(4 + (y + k) % 4)
        count = TOK if k < 2 else HALF
        sem = k if k < 2 else 2 * k - 2 + h
        src = v_ref if k == 0 else at(row + h * HALF, count)
        return remote(src, at(their + h * HALF, count), f_send.at[sem], f_recv.at[sem], cross[0])

    def halves(k):
        return (0,) if k < 2 else (0, 1)

    def tag_copy(k):
        own_tags, near_tags = tag_row(own_row), tag_row(near_row)
        src, dst, to = [
            (d_ref, tag_at(own_tags, TAG_ROWS), ahead),
            (tag_at(near_tags, TAG_ROWS), tag_at(near_tags, TAG_ROWS), ahead),
            (d_ref, tag_at(own_tags, TAG_ROWS), mates[0]),
            (d_ref.at[pl.ds(0, HALF_TAGS)], tag_at(0, HALF_TAGS), far[0]),
            (d_ref.at[pl.ds(HALF_TAGS, HALF_TAGS)], tag_at(0, HALF_TAGS), far_partner[0]),
            (tag_at(0, HALF_TAGS), tag_at(HALF_TAGS, HALF_TAGS), place(x + dx, zh, y)),
        ][k]
        return remote(src, dst, t_send.at[k], t_recv.at[min(k, 3) if k < 5 else 4], to)

    def tag_forward(k):
        src = d_ref if k == 0 else tag_at(tag_row(block((y + k) % 4)), TAG_ROWS)
        return remote(src, tag_at(tag_row(block(4 + (y + k) % 4)), TAG_ROWS), t_send.at[6 + k], t_recv.at[5 + k], cross[0])

    own_v = pltpu.make_async_copy(v_ref, at(own_row, TOK), own_sem.at[0])
    own_d = pltpu.make_async_copy(d_ref, tag_at(tag_row(own_row), TAG_ROWS), own_sem.at[1])

    def widen(row, count):
        shape = (LANES, LANES)
        eye = lax.broadcasted_iota(jnp.int32, shape, 0) == lax.broadcasted_iota(jnp.int32, shape, 1)
        labels = tags[pl.ds(pl.multiple_of(tag_row(row), 8), count // LANES), :].astype(jnp.float32)
        spread = jnp.concatenate(
            [
                jnp.where(eye, jnp.broadcast_to(labels[q : q + 1, :], shape), 0.0).astype(jnp.bfloat16)
                for q in range(count // LANES)
            ],
            axis=0,
        )
        wide[pl.ds(pl.multiple_of(row, LANES), count), :] = jnp.dot(
            spread, jnp.ones(shape, jnp.bfloat16), preferred_element_type=jnp.float32
        )

    def tile(left, right, first, body=BODY):
        spot = pl.ds(pl.multiple_of(left, LANES), body)
        labels = tags[pl.ds(pl.multiple_of(tag_row(right), 8), TAG_ROWS), :].astype(jnp.float32)
        b = (right - GROUP) // TOK
        for w in range(TOK // WIDTH):
            scores = lax.dot_general(
                buf[spot, :], buf[pl.ds(pl.multiple_of(right + w * WIDTH, WIDTH), WIDTH), :],
                (((1,), (1,)), ((), ())), preferred_element_type=jnp.float32,
            )
            marks = wide[spot, :]
            best = None if first and w == 0 else rows[spot, :]
            for k in range(WIDTH // LANES):
                q = w * (WIDTH // LANES) + k
                part = jnp.where(marks == labels[q : q + 1, :], NEG, scores[:, k * LANES : (k + 1) * LANES])
                best = part if best is None else jnp.maximum(best, part)
                peak = jnp.max(part.reshape(body // 8, 8, LANES), axis=0)
                lanes = slice(q * LANES, (q + 1) * LANES)
                cols[b, :, lanes] = jnp.maximum(cols[b, :, lanes], peak)
            rows[spot, :] = best

    def row_peaks(row, count):
        part = rows[pl.ds(pl.multiple_of(row, LANES), count), :]
        return jnp.max(part.reshape(count // LANES, LANES, LANES), axis=2)

    def col_peaks(b):
        return jnp.concatenate(
            [jnp.max(cols[b, :, q * LANES : (q + 1) * LANES], axis=0, keepdims=True) for q in range(TAG_ROWS)], axis=0
        )

    def message(src, count, dst, send, recv, to):
        slot, start = dst
        return remote(
            res.at[pl.ds(pl.multiple_of(src, 8), count)], ret.at[slot, pl.ds(start, count)],
            m_send.at[send], m_recv.at[recv], to,
        )

    def res_row(b):
        return pl.multiple_of(tag_row(block(b)), TAG_ROWS)

    late = jnp.where(y < 2, two, y)
    early = jnp.where(y < 2, y, two)
    late_row = block(late) + jnp.where(y < 2, 0, HALF)
    minus = jnp.where(zh == 1, DIRECT, RELAYED)
    plus = jnp.where(zh == 1, RELAYED, DIRECT)
    center = block(group + y)

    def start_b(c):
        if c == 0:
            tag_copy(2).start()
        b_copy(c).start()

    own_v.start()
    own_d.start()

    with scope("hello"):
        @pl.when(takes)
        def _():
            hello([far[0], feeder, *mates, *cross], 5)
            tag_copy(0).start()
            for c in range(Y_PIECES):
                a_copy(c).start()
            tag_forward(0).start()
            forward(0).start()

            @pl.when(zh == 0)
            def _():
                for c in range(Y_PIECES):
                    start_b(c)

        @pl.when(gives)
        def _():
            hello([far_partner[0], feeder, *mates, cross[0]], 10)
            tag_copy(3).start()
            tag_copy(4).start()
            for j in range(Z_PIECES):
                z_copy(0, j).start()
                z_copy(1, j).start()
                if j == 0:
                    tag_copy(0).start()
                if j % 2 == 1:
                    a_copy(j // 2).start()

    with scope("init"):
        cols[...] = jnp.full(cols.shape, NEG, jnp.float32)
        res[...] = jnp.full(res.shape, NEG, jnp.float32)
        own_v.wait()
        own_d.wait()
        widen(own_row, TOK)

    def pass_on(c, do):
        if c < Y_PIECES // 2:
            getattr(c_copy(c), do)()
        else:
            whole = takes | ((y >= 2) if do == "wait_recv" else (y == 1) | (y == 2))

            @pl.when(whole)
            def _():
                getattr(c_copy(c), do)()

    def on_near(c):
        with scope("near%d" % c):
            if c == 0:
                tag_copy(0).wait_recv()
                widen(near_row, TOK)
            a_copy(c).wait_recv()
            tile(near_row + c * Y_ROWS, own_row, True)

    def on_receiver_near(c):
        a_copy(c).wait_recv()
        c_copy(c).start()
        if c == Y_PIECES - 1:
            tag_forward(1).start()
            forward(1).start()

        @pl.when(zh == 1)
        def _():
            start_b(c)

        tile(near_row + c * Y_ROWS, own_row, True)

    def on_z(j):
        with scope("z%d" % j):
            if j == 0:
                tag_copy(3).wait_recv()
                tag_copy(5).start()
            for piece in (2 * j, 2 * j + 1):
                z_copy(0, piece).wait_recv()
                r_copy(piece).start()

    def on_direct(i):
        with scope("dir%d" % i):
            if i == 0:
                @pl.when(gives)
                def _():
                    tag_forward(0).wait_recv()
                    forward(0).wait_recv()
                tag_copy(5).wait_recv()
                widen(DIRECT, TOK)
            start, count = GROUPS[i]
            tile(DIRECT + start, center, True, count)

    def on_two(h):
        with scope("two%d" % h):
            @pl.when(takes)
            def _():
                if h == 0:
                    tag_copy(1).wait_recv()
                    tag_forward(2).start()
                for c in (2 * h, 2 * h + 1):
                    c_copy(c).wait_recv()
                forward(2, h).start()

    def on_down(h):
        with scope("down%d" % h):
            @pl.when(takes)
            def _():
                if h == 0:
                    tag_copy(2).wait_recv()
                    tag_forward(3).start()
                for c in (2 * h, 2 * h + 1):
                    b_copy(c).wait_recv()
                forward(3, h).start()

    def others(i, ks):
        start, count = GROUPS[i]
        for k in ks:
            if i == 0:
                @pl.when(gives)
                def _():
                    tag_forward(k).wait_recv()
                    for h in halves(k):
                        forward(k, h).wait_recv()

            b = (y + k) % 4
            tile(jnp.where(b > y, plus, minus) + start, block(group + b), False, count)

    def on_relayed(i):
        start, count = GROUPS[i]
        for j in range(start // Z_ROWS, (start + count) // Z_ROWS):
            r_copy(j).wait_recv()
        tile(RELAYED + start, center, True, count)

    @pl.when(takes)
    def _():
        with scope("recv01"):
            tag_copy(0).wait_recv()
            tag_copy(1).start()
            widen(near_row, TOK)
            on_receiver_near(0)
            on_receiver_near(1)

    on_z(0)

    @pl.when(takes)
    def _():
        with scope("recv23"):
            on_receiver_near(2)
            on_receiver_near(3)

    @pl.when(gives)
    def _():
        on_near(0)
        on_near(1)

    on_z(1)
    on_direct(0)

    @pl.when(gives)
    def _():
        tag_copy(1).start()
        pass_on(0, "start")
        pass_on(1, "start")
        for c in (2, 3):
            with scope("near%d" % c):
                a_copy(c).wait_recv()
                pass_on(c, "start")
                tile(near_row + c * Y_ROWS, own_row, True)

    on_z(2)

    @pl.when(gives)
    def _():
        with scope("adj"):
            res[pl.ds(res_row(near), TAG_ROWS), :] = row_peaks(near_row, TOK)
            message(res_row(near), TAG_ROWS, (2, 0), 2, 4, mates[2]).start()

    on_two(0)
    on_direct(1)
    with scope("rel0"):
        on_relayed(0)
    on_two(1)
    on_down(0)
    with scope("oth0a"):
        others(0, (1,))
    on_down(1)
    on_z(3)
    with scope("oth0b"):
        others(0, (2,))

    with scope("oth0c"):
        others(0, (3,))
    with scope("rel1"):
        on_relayed(1)
    with scope("oth1"):
        others(1, (1, 2, 3))
    on_direct(2)
    with scope("rel2"):
        on_relayed(2)
    with scope("oth2"):
        others(2, (1, 2, 3))

    with scope("zpeaks"):
        res[HALF_TAGS:TAG_ROWS, :] = row_peaks(RELAYED, HALF)

        @pl.when(takes)
        def _():
            message(HALF_TAGS, HALF_TAGS, (1, 0), 1, 2, far[1]).start()

        @pl.when(gives)
        def _():
            message(HALF_TAGS, HALF_TAGS, (1, HALF_TAGS), 1, 3, far_partner[1]).start()

        res[0:HALF_TAGS, :] = row_peaks(DIRECT, HALF)

        @pl.when(takes)
        def _():
            message(0, HALF_TAGS, (0, 0), 0, 0, far[0]).start()

        @pl.when(gives)
        def _():
            message(0, HALF_TAGS, (0, HALF_TAGS), 0, 1, far_partner[0]).start()
            for k in (1, 2, 3, 0):
                b = 4 + (y + k) % 4
                slot = 3 + (4 - k) % 4
                res[pl.ds(res_row(b), TAG_ROWS), :] = col_peaks(b)
                message(res_row(b), TAG_ROWS, (slot, 0), 4 + k, slot, cross[k]).start()

    def settle(k):
        spot = pl.ds(res_row((y + k) % 4), TAG_ROWS)
        res[spot, :] = jnp.maximum(res[spot, :], col_peaks((y + k) % 4))

    def to_mate(k):
        settle(k)
        message(res_row((y + k) % 4), TAG_ROWS, (3 - k, 0), 1 + k, 3 - k, mates[k - 1]).start()

    @pl.when(takes)
    def _():
        with scope("rpeaks"):
            res[pl.ds(res_row(near), TAG_ROWS), :] = row_peaks(near_row, TOK)
            to_mate(1)
            to_mate(3)

    with scope("opp"):
        @pl.when(gives)
        def _():
            tag_copy(1).wait_recv()
            for c in range(Y_PIECES):
                pass_on(c, "wait_recv")

        widen(two_row, TOK)
        tile(late_row, block(early), True)
        tile(late_row + BODY, block(early), True)

    with scope("peaks"):
        res[pl.ds(pl.multiple_of(tag_row(late_row), HALF_TAGS), HALF_TAGS), :] = row_peaks(late_row, HALF)

        @pl.when(takes)
        def _():
            to_mate(2)

        @pl.when(gives)
        def _():
            settle(2)
            message(res_row(two), TAG_ROWS, (3, 0), 3, 5, mates[1]).start()

        settle(0)

    with scope("final"):
        @pl.when(takes)
        def _():
            best = res[pl.ds(res_row(y), TAG_ROWS), :]
            for slot in range(7):
                message(0, TAG_ROWS, (slot, 0), 0, slot, mates[0]).wait_recv()
                best = jnp.maximum(best, ret[slot])
            o_ref[...] = best

        @pl.when(gives)
        def _():
            best = res[pl.ds(res_row(y), TAG_ROWS), :]
            for slot in (2, 3):
                message(0, TAG_ROWS, (slot, 0), 0, slot + 2, mates[0]).wait_recv()
                best = jnp.maximum(best, ret[slot])
            for sem in range(4):
                message(0, HALF_TAGS, (0, 0), 0, sem, mates[0]).wait_recv()
            for slot in (0, 1):
                best = jnp.maximum(best, ret[slot])
            o_ref[...] = best

    with scope("drain"):
        for c in range(Y_PIECES):
            a_copy(c).wait_send()
            pass_on(c, "wait_send")
        for j in range(Z_PIECES):
            r_copy(j).wait_send()
        for k in (0, 1, 5):
            tag_copy(k).wait_send()

        @pl.when(takes)
        def _():
            for c in range(Y_PIECES):
                b_copy(c).wait_send()
            tag_copy(2).wait_send()
            for k in range(4):
                for h in halves(k):
                    forward(k, h).wait_send()
                tag_forward(k).wait_send()
            for sem in range(5):
                message(0, HALF_TAGS if sem < 2 else TAG_ROWS, (0, 0), sem, 0, mates[0]).wait_send()

        @pl.when(gives)
        def _():
            for j in range(Z_PIECES):
                z_copy(0, j).wait_send()
                z_copy(1, j).wait_send()
            tag_copy(3).wait_send()
            tag_copy(4).wait_send()
            for sem in range(8):
                message(0, HALF_TAGS if sem < 2 else TAG_ROWS, (0, 0), sem, 0, mates[0]).wait_send()


def per_device(vectors, docs, prior):
    dma = pltpu.SemaphoreType.DMA
    found = pl.pallas_call(
        kernel,
        out_shape=pltpu.VMEM((TAG_ROWS, LANES), jnp.float32),
        in_specs=[pl.BlockSpec(memory_space=pl.ANY)] * 2,
        out_specs=pl.BlockSpec(memory_space=pltpu.VMEM),
        scratch_shapes=[
            pltpu.VMEM((BLOCK_ROWS, DIM), jnp.bfloat16),
            pltpu.VMEM((BLOCK_ROWS // LANES, LANES), jnp.int32),
            pltpu.VMEM((LEFT_ROWS, LANES), jnp.float32),
            pltpu.VMEM((LEFT_ROWS, LANES), jnp.float32),
            pltpu.VMEM((8, 8, TOK), jnp.float32),
            pltpu.VMEM((BLOCK_ROWS // LANES, LANES), jnp.float32),
            pltpu.VMEM((7, TAG_ROWS, LANES), jnp.float32),
            dma((2,)),
            dma((Y_PIECES,)), dma((Y_PIECES,)),
            dma((Y_PIECES,)), dma((Y_PIECES,)),
            dma((Y_PIECES,)), dma((Y_PIECES,)),
            dma((6,)), dma((6,)),
            dma((2 * Z_PIECES,)), dma((Z_PIECES,)),
            dma((Z_PIECES,)), dma((Z_PIECES,)),
            dma((10,)), dma((9,)),
            dma((8,)), dma((7,)),
        ],
        compiler_params=pltpu.CompilerParams(collective_id=0, has_side_effects=True),
        name="window",
    )(vectors, docs.reshape(TAG_ROWS, LANES))
    return jnp.maximum(prior, found.reshape(TOK))


def solution(mesh):
    return jax.shard_map(
        per_device,
        mesh=mesh,
        in_specs=(P(("slab", "corpus"), None), P(("slab", "corpus")), P(("slab", "corpus"))),
        out_specs=P(("slab", "corpus")),
        check_vma=False,
    )
```

```python
import jax
import jax.numpy as jnp
from jax import lax
from jax.experimental import pallas as pl
from jax.experimental.pallas import tpu as pltpu
from jax.sharding import PartitionSpec as P

MESH = pl.DeviceIdType.MESH
NEG = -1e30
TOK = 2048
HALF = TOK // 2
DIM = 128
LANES = 128
TAG_ROWS = TOK // LANES
HALF_TAGS = TAG_ROWS // 2
Z_PIECES = 4
Z_ROWS = HALF // Z_PIECES
Y_PIECES = 4
Y_ROWS = TOK // Y_PIECES
BODY = 512
GROUPS = ((0, 512), (512, 256), (768, 256))
WIDTH = 512
DIRECT, RELAYED, GROUP = 0, HALF, TOK
BLOCK_ROWS = TOK + 8 * TOK
LEFT_ROWS = TOK + 4 * TOK


def scope(name):
    return jax.named_scope(name)


def kernel(
    v_ref, d_ref, o_ref,
    buf, tags, wide, rows, cols, res, ret,
    own_sem, a_send, a_recv, c_send, c_recv, b_send, b_recv, f_send, f_recv, z_send, z_recv, r_send, r_recv,
    t_send, t_recv, m_send, m_recv,
):
    slab, corpus = lax.axis_index("slab"), lax.axis_index("corpus")
    x, zh, y = corpus // 8, (corpus // 4) % 2, corpus % 4
    core = slab % 2
    takes = (zh + core) % 2 == 1
    gives = (zh + core) % 2 == 0
    half = (zh + core + 1) % 2
    partner = slab + 1 - 2 * core
    other = 1 - zh
    dx = 1 - 2 * zh

    def place(px, pz, py, s=slab):
        return (s, ((px + 4) % 4) * 8 + pz * 4 + (py + 4) % 4)

    def block(b):
        return pl.multiple_of(GROUP + b * TOK, TOK)

    def remote(src, dst, send, recv, to):
        return pltpu.make_async_remote_copy(
            src_ref=src, dst_ref=dst, send_sem=send, recv_sem=recv, device_id=to, device_id_type=MESH
        )

    def at(start, count):
        return buf.at[pl.ds(pl.multiple_of(start, 16), count)]

    def tag_at(start, count):
        return tags.at[pl.ds(pl.multiple_of(start, 8), count)]

    def tag_row(row):
        return row // LANES

    up, two, down = (y + 1) % 4, (y + 2) % 4, (y + 3) % 4
    near = jnp.where(takes, up, down)
    ahead = place(x, zh, jnp.where(takes, y - 1, y + 1))
    group = jnp.where(takes, 0, 4)
    own_row, near_row, two_row = block(y), block(near), block(two)

    barrier = pltpu.get_barrier_semaphore()

    def hello(greeted, awaited):
        for to in greeted:
            pl.semaphore_signal(barrier, inc=1, device_id=to, device_id_type=MESH)
        pl.semaphore_wait(barrier, awaited)

    mates = [place(x, zh, y + k) for k in (1, 2, 3)]
    cross = [place(x, zh, y + k, partner) for k in (0, 1, 2, 3)]
    feeder = place(x - dx, zh, y)
    far = [place(x, other, y), place(x - dx, other, y)]
    far_partner = [place(x, other, y, partner), place(x - dx, other, y, partner)]

    def a_copy(c):
        return remote(
            v_ref.at[pl.ds(c * Y_ROWS, Y_ROWS)], at(own_row + c * Y_ROWS, Y_ROWS), a_send.at[c], a_recv.at[c], ahead
        )

    def c_copy(c):
        spot = at(near_row + c * Y_ROWS, Y_ROWS)
        return remote(spot, spot, c_send.at[c], c_recv.at[c], ahead)

    def b_copy(c):
        return remote(
            v_ref.at[pl.ds(c * Y_ROWS, Y_ROWS)], at(own_row + c * Y_ROWS, Y_ROWS), b_send.at[c], b_recv.at[c], mates[0]
        )


    def z_copy(h, j):
        return remote(
            v_ref.at[pl.ds(h * HALF + j * Z_ROWS, Z_ROWS)], at(DIRECT + j * Z_ROWS, Z_ROWS),
            z_send.at[h * Z_PIECES + j], z_recv.at[j], (far if h == 0 else far_partner)[0],
        )

    def r_copy(j):
        return remote(
            at(DIRECT + j * Z_ROWS, Z_ROWS), at(RELAYED + j * Z_ROWS, Z_ROWS), r_send.at[j], r_recv.at[j],
            place(x + dx, zh, y),
        )

    def forward(k, h=0):
        row, their = block((y + k) % 4), block(4 + (y + k) % 4)
        count = TOK if k < 2 else HALF
        sem = k if k < 2 else 2 * k - 2 + h
        src = v_ref if k == 0 else at(row + h * HALF, count)
        return remote(src, at(their + h * HALF, count), f_send.at[sem], f_recv.at[sem], cross[0])

    def halves(k):
        return (0,) if k < 2 else (0, 1)

    def tag_copy(k):
        own_tags, near_tags = tag_row(own_row), tag_row(near_row)
        src, dst, to = [
            (d_ref, tag_at(own_tags, TAG_ROWS), ahead),
            (tag_at(near_tags, TAG_ROWS), tag_at(near_tags, TAG_ROWS), ahead),
            (d_ref, tag_at(own_tags, TAG_ROWS), mates[0]),
            (d_ref.at[pl.ds(0, HALF_TAGS)], tag_at(0, HALF_TAGS), far[0]),
            (d_ref.at[pl.ds(HALF_TAGS, HALF_TAGS)], tag_at(0, HALF_TAGS), far_partner[0]),
            (tag_at(0, HALF_TAGS), tag_at(HALF_TAGS, HALF_TAGS), place(x + dx, zh, y)),
        ][k]
        return remote(src, dst, t_send.at[k], t_recv.at[min(k, 3) if k < 5 else 4], to)

    def tag_forward(k):
        src = d_ref if k == 0 else tag_at(tag_row(block((y + k) % 4)), TAG_ROWS)
        return remote(src, tag_at(tag_row(block(4 + (y + k) % 4)), TAG_ROWS), t_send.at[6 + k], t_recv.at[5 + k], cross[0])

    own_v = pltpu.make_async_copy(v_ref, at(own_row, TOK), own_sem.at[0])
    own_d = pltpu.make_async_copy(d_ref, tag_at(tag_row(own_row), TAG_ROWS), own_sem.at[1])

    def widen(row, count):
        shape = (LANES, LANES)
        eye = lax.broadcasted_iota(jnp.int32, shape, 0) == lax.broadcasted_iota(jnp.int32, shape, 1)
        labels = tags[pl.ds(pl.multiple_of(tag_row(row), 8), count // LANES), :].astype(jnp.float32)
        spread = jnp.concatenate(
            [
                jnp.where(eye, jnp.broadcast_to(labels[q : q + 1, :], shape), 0.0).astype(jnp.bfloat16)
                for q in range(count // LANES)
            ],
            axis=0,
        )
        wide[pl.ds(pl.multiple_of(row, LANES), count), :] = jnp.dot(
            spread, jnp.ones(shape, jnp.bfloat16), preferred_element_type=jnp.float32
        )

    def tile(left, right, first, body=BODY):
        spot = pl.ds(pl.multiple_of(left, body), body)
        labels = tags[pl.ds(pl.multiple_of(tag_row(right), 8), TAG_ROWS), :].astype(jnp.float32)
        b = (right - GROUP) // TOK
        for w in range(TOK // WIDTH):
            scores = lax.dot_general(
                buf[spot, :], buf[pl.ds(pl.multiple_of(right + w * WIDTH, WIDTH), WIDTH), :],
                (((1,), (1,)), ((), ())), preferred_element_type=jnp.float32,
            )
            marks = wide[spot, :]
            best = None if first and w == 0 else rows[spot, :]
            for k in range(WIDTH // LANES):
                q = w * (WIDTH // LANES) + k
                part = jnp.where(marks == labels[q : q + 1, :], NEG, scores[:, k * LANES : (k + 1) * LANES])
                best = part if best is None else jnp.maximum(best, part)
                peak = jnp.max(part.reshape(body // 8, 8, LANES), axis=0)
                lanes = slice(q * LANES, (q + 1) * LANES)
                cols[b, :, lanes] = jnp.maximum(cols[b, :, lanes], peak)
            rows[spot, :] = best

    def row_peaks(row, count):
        part = rows[pl.ds(pl.multiple_of(row, LANES), count), :]
        return jnp.max(part.reshape(count // LANES, LANES, LANES), axis=2)

    def col_peaks(b):
        return jnp.concatenate(
            [jnp.max(cols[b, :, q * LANES : (q + 1) * LANES], axis=0, keepdims=True) for q in range(TAG_ROWS)], axis=0
        )

    def message(src, count, dst, send, recv, to):
        slot, start = dst
        return remote(
            res.at[pl.ds(pl.multiple_of(src, 8), count)], ret.at[slot, pl.ds(start, count)],
            m_send.at[send], m_recv.at[recv], to,
        )

    def res_row(b):
        return pl.multiple_of(tag_row(block(b)), TAG_ROWS)

    late = jnp.where(y < 2, two, y)
    early = jnp.where(y < 2, y, two)
    late_row = block(late) + jnp.where(y < 2, 0, HALF)
    minus = jnp.where(zh == 1, DIRECT, RELAYED)
    plus = jnp.where(zh == 1, RELAYED, DIRECT)
    center = block(group + y)

    def start_b(c):
        if c == 0:
            tag_copy(2).start()
        b_copy(c).start()

    own_v.start()
    own_d.start()

    with scope("hello"):
        @pl.when(takes)
        def _():
            hello([far[0], feeder, *mates, *cross], 5)
            tag_copy(0).start()
            for c in range(Y_PIECES):
                a_copy(c).start()
            tag_forward(0).start()
            forward(0).start()

            @pl.when(zh == 0)
            def _():
                for c in range(Y_PIECES):
                    start_b(c)

        @pl.when(gives)
        def _():
            hello([far_partner[0], feeder, *mates, cross[0]], 10)
            tag_copy(3).start()
            tag_copy(4).start()
            for j in range(Z_PIECES):
                z_copy(0, j).start()
                z_copy(1, j).start()
            tag_copy(0).start()
            for c in range(Y_PIECES):
                a_copy(c).start()

    with scope("init"):
        cols[...] = jnp.full(cols.shape, NEG, jnp.float32)
        res[...] = jnp.full(res.shape, NEG, jnp.float32)
        own_v.wait()
        own_d.wait()
        widen(own_row, TOK)

    def pass_on(c, do):
        if c < Y_PIECES // 2:
            getattr(c_copy(c), do)()
        else:
            whole = takes | ((y >= 2) if do == "wait_recv" else (y == 1) | (y == 2))

            @pl.when(whole)
            def _():
                getattr(c_copy(c), do)()

    def on_near(c):
        with scope("near%d" % c):
            if c == 0:
                tag_copy(0).wait_recv()
                widen(near_row, TOK)
            a_copy(c).wait_recv()
            tile(near_row + c * Y_ROWS, own_row, True)

    def on_receiver_near(c):
        a_copy(c).wait_recv()
        c_copy(c).start()
        if c == Y_PIECES - 1:
            tag_forward(1).start()
            forward(1).start()

        @pl.when(zh == 1)
        def _():
            start_b(c)

        tile(near_row + c * Y_ROWS, own_row, True)

    def on_z(j):
        with scope("z%d" % j):
            if j == 0:
                tag_copy(3).wait_recv()
                tag_copy(5).start()
            z_copy(0, j).wait_recv()
            r_copy(j).start()

    def on_direct(i):
        with scope("dir%d" % i):
            if i == 0:
                @pl.when(gives)
                def _():
                    tag_forward(0).wait_recv()
                    forward(0).wait_recv()
                tag_copy(5).wait_recv()
                widen(DIRECT, TOK)
            start, count = GROUPS[i]
            tile(DIRECT + start, center, True, count)

    def on_two(h):
        with scope("two%d" % h):
            @pl.when(takes)
            def _():
                if h == 0:
                    tag_copy(1).wait_recv()
                    tag_forward(2).start()
                for c in (2 * h, 2 * h + 1):
                    c_copy(c).wait_recv()
                forward(2, h).start()

    def on_down(h):
        with scope("down%d" % h):
            @pl.when(takes)
            def _():
                if h == 0:
                    tag_copy(2).wait_recv()
                    tag_forward(3).start()
                for c in (2 * h, 2 * h + 1):
                    b_copy(c).wait_recv()
                forward(3, h).start()

    def others(i, ks):
        start, count = GROUPS[i]
        for k in ks:
            if i == 0:
                @pl.when(gives)
                def _():
                    tag_forward(k).wait_recv()
                    for h in halves(k):
                        forward(k, h).wait_recv()

            b = (y + k) % 4
            tile(jnp.where(b > y, plus, minus) + start, block(group + b), False, count)

    def on_relayed(i):
        start, count = GROUPS[i]
        for j in range(start // Z_ROWS, (start + count) // Z_ROWS):
            r_copy(j).wait_recv()
        tile(RELAYED + start, center, True, count)

    @pl.when(takes)
    def _():
        with scope("recv01"):
            tag_copy(0).wait_recv()
            tag_copy(1).start()
            widen(near_row, TOK)
            on_receiver_near(0)
            on_receiver_near(1)

    on_z(0)

    @pl.when(takes)
    def _():
        with scope("recv23"):
            on_receiver_near(2)
            on_receiver_near(3)

    @pl.when(gives)
    def _():
        on_near(0)
        on_near(1)

    on_z(1)
    on_direct(0)

    @pl.when(gives)
    def _():
        tag_copy(1).start()
        pass_on(0, "start")
        pass_on(1, "start")
        for c in (2, 3):
            with scope("near%d" % c):
                a_copy(c).wait_recv()
                pass_on(c, "start")
                tile(near_row + c * Y_ROWS, own_row, True)

    on_z(2)

    @pl.when(gives)
    def _():
        with scope("adj"):
            res[pl.ds(res_row(near), TAG_ROWS), :] = row_peaks(near_row, TOK)
            message(res_row(near), TAG_ROWS, (2, 0), 2, 4, mates[2]).start()

    on_two(0)
    on_direct(1)
    with scope("rel0"):
        on_relayed(0)
    on_two(1)
    on_down(0)
    with scope("oth0a"):
        others(0, (1,))
    on_down(1)
    on_z(3)
    with scope("oth0b"):
        others(0, (2,))

    with scope("oth0c"):
        others(0, (3,))
    with scope("rel1"):
        on_relayed(1)
    with scope("oth1"):
        others(1, (1, 2, 3))
    on_direct(2)
    with scope("rel2"):
        on_relayed(2)
    with scope("oth2"):
        others(2, (1, 2, 3))

    with scope("zpeaks"):
        res[HALF_TAGS:TAG_ROWS, :] = row_peaks(RELAYED, HALF)

        @pl.when(takes)
        def _():
            message(HALF_TAGS, HALF_TAGS, (1, 0), 1, 2, far[1]).start()

        @pl.when(gives)
        def _():
            message(HALF_TAGS, HALF_TAGS, (1, HALF_TAGS), 1, 3, far_partner[1]).start()

        res[0:HALF_TAGS, :] = row_peaks(DIRECT, HALF)

        @pl.when(takes)
        def _():
            message(0, HALF_TAGS, (0, 0), 0, 0, far[0]).start()

        @pl.when(gives)
        def _():
            message(0, HALF_TAGS, (0, HALF_TAGS), 0, 1, far_partner[0]).start()
            for k in (1, 2, 3, 0):
                b = 4 + (y + k) % 4
                slot = 3 + (4 - k) % 4
                res[pl.ds(res_row(b), TAG_ROWS), :] = col_peaks(b)
                message(res_row(b), TAG_ROWS, (slot, 0), 4 + k, slot, cross[k]).start()

    def settle(k):
        spot = pl.ds(res_row((y + k) % 4), TAG_ROWS)
        res[spot, :] = jnp.maximum(res[spot, :], col_peaks((y + k) % 4))

    def to_mate(k):
        settle(k)
        message(res_row((y + k) % 4), TAG_ROWS, (3 - k, 0), 1 + k, 3 - k, mates[k - 1]).start()

    @pl.when(takes)
    def _():
        with scope("rpeaks"):
            res[pl.ds(res_row(near), TAG_ROWS), :] = row_peaks(near_row, TOK)
            to_mate(1)
            to_mate(3)

    with scope("opp"):
        @pl.when(gives)
        def _():
            tag_copy(1).wait_recv()
            for c in range(Y_PIECES):
                pass_on(c, "wait_recv")

        widen(two_row, TOK)
        tile(late_row, block(early), True)
        tile(late_row + BODY, block(early), True)

    with scope("peaks"):
        res[pl.ds(pl.multiple_of(tag_row(late_row), HALF_TAGS), HALF_TAGS), :] = row_peaks(late_row, HALF)

        @pl.when(takes)
        def _():
            to_mate(2)

        @pl.when(gives)
        def _():
            settle(2)
            message(res_row(two), TAG_ROWS, (3, 0), 3, 5, mates[1]).start()

        settle(0)

    with scope("final"):
        @pl.when(takes)
        def _():
            best = res[pl.ds(res_row(y), TAG_ROWS), :]
            for slot in range(7):
                message(0, TAG_ROWS, (slot, 0), 0, slot, mates[0]).wait_recv()
                best = jnp.maximum(best, ret[slot])
            o_ref[...] = best

        @pl.when(gives)
        def _():
            best = res[pl.ds(res_row(y), TAG_ROWS), :]
            for slot in (2, 3):
                message(0, TAG_ROWS, (slot, 0), 0, slot + 2, mates[0]).wait_recv()
                best = jnp.maximum(best, ret[slot])
            for sem in range(4):
                message(0, HALF_TAGS, (0, 0), 0, sem, mates[0]).wait_recv()
            for slot in (0, 1):
                best = jnp.maximum(best, ret[slot])
            o_ref[...] = best

    with scope("drain"):
        for c in range(Y_PIECES):
            a_copy(c).wait_send()
            pass_on(c, "wait_send")
        for j in range(Z_PIECES):
            r_copy(j).wait_send()
        for k in (0, 1, 5):
            tag_copy(k).wait_send()

        @pl.when(takes)
        def _():
            for c in range(Y_PIECES):
                b_copy(c).wait_send()
            tag_copy(2).wait_send()
            for k in range(4):
                for h in halves(k):
                    forward(k, h).wait_send()
                tag_forward(k).wait_send()
            for sem in range(5):
                message(0, HALF_TAGS if sem < 2 else TAG_ROWS, (0, 0), sem, 0, mates[0]).wait_send()

        @pl.when(gives)
        def _():
            for j in range(Z_PIECES):
                z_copy(0, j).wait_send()
                z_copy(1, j).wait_send()
            tag_copy(3).wait_send()
            tag_copy(4).wait_send()
            for sem in range(8):
                message(0, HALF_TAGS if sem < 2 else TAG_ROWS, (0, 0), sem, 0, mates[0]).wait_send()


def per_device(vectors, docs, prior):
    dma = pltpu.SemaphoreType.DMA
    found = pl.pallas_call(
        kernel,
        out_shape=pltpu.VMEM((TAG_ROWS, LANES), jnp.float32),
        in_specs=[pl.BlockSpec(memory_space=pl.ANY)] * 2,
        out_specs=pl.BlockSpec(memory_space=pltpu.VMEM),
        scratch_shapes=[
            pltpu.VMEM((BLOCK_ROWS, DIM), jnp.bfloat16),
            pltpu.VMEM((BLOCK_ROWS // LANES, LANES), jnp.int32),
            pltpu.VMEM((LEFT_ROWS, LANES), jnp.float32),
            pltpu.VMEM((LEFT_ROWS, LANES), jnp.float32),
            pltpu.VMEM((8, 8, TOK), jnp.float32),
            pltpu.VMEM((BLOCK_ROWS // LANES, LANES), jnp.float32),
            pltpu.VMEM((7, TAG_ROWS, LANES), jnp.float32),
            dma((2,)),
            dma((Y_PIECES,)), dma((Y_PIECES,)),
            dma((Y_PIECES,)), dma((Y_PIECES,)),
            dma((Y_PIECES,)), dma((Y_PIECES,)),
            dma((6,)), dma((6,)),
            dma((2 * Z_PIECES,)), dma((Z_PIECES,)),
            dma((Z_PIECES,)), dma((Z_PIECES,)),
            dma((10,)), dma((9,)),
            dma((8,)), dma((7,)),
        ],
        compiler_params=pltpu.CompilerParams(collective_id=0, has_side_effects=True),
        name="window",
    )(vectors, docs.reshape(TAG_ROWS, LANES))
    return jnp.maximum(prior, found.reshape(TOK))


def solution(mesh):
    return jax.shard_map(
        per_device,
        mesh=mesh,
        in_specs=(P(("slab", "corpus"), None), P(("slab", "corpus")), P(("slab", "corpus"))),
        out_specs=P(("slab", "corpus")),
        check_vma=False,
    )
```
